32 devices in a mesh: row: 4 (over y, x), col: 8 (over z, core).
Axes of the slice: x: 2, y: 2, z: 4, core: 2. Of those that a mesh axis runs over, the one named last changes fastest.
Arguments:
- factor: bfloat16 [4096, 131072], P('row', 'col'), may hold values from -0.015625 to 0.015625
- panels: bfloat16 [131072, 256], P('col', 'row'), may hold values from -6 to 6
- base_demand: float32 [4096], replicated, may hold values from 0.3 to 3
- spread: float32 [4096], replicated, may hold values from 0.1 to 0.6
- head_base: float32 [4096], replicated, may hold values from -8 to 8
- head_drop: float32 [4096], replicated, may hold values from 0.2 to 1
- conductance: float32 [8192], replicated, may hold values from 0.3 to 1.5
- pipe_ends: int32 [8192, 2], replicated, may hold values from 0 to 4095
Outputs:
- imbalance: float32 [256, 4096], P(('col', 'row'))
The draws below stay inside these ranges and needn't reach their ends.
All inputs are finite; a program needn't handle non-finite values.
Results may differ from the reference program's by a relative error of at most 0.0003.
Values may be sent and summed in bfloat16 or wider, within the bound.
A program may use at most 128 MiB of HBM per device.

```python
import math
import jax
import jax.numpy as jnp
from jax import lax

NODES = 131072
SLAB = 4096
SCENARIOS = 256
PIPES = 8192
N_COL = 8


def place_ends(entries, key, least, high):
    spot = [jax.random.randint(jax.random.fold_in(key, axis), (), 0, length) for axis, length in enumerate(entries.shape)]
    longest = entries.shape.index(max(entries.shape))
    next_to = spot[:longest] + [(spot[longest] + 1) % entries.shape[longest]] + spot[longest + 1:]
    return entries.at[tuple(spot)].set(least).at[tuple(next_to)].set(high)


def shard_levels(own_key, shape, cuts, least, largest):
    level = 1.0
    for axis_at, blocks in cuts:
        steps = jax.random.uniform(jax.random.fold_in(jax.random.fold_in(own_key, 6), axis_at), (blocks,), jnp.float32, least / len(cuts), largest / len(cuts))
        level = level * jnp.repeat(jnp.exp(steps), shape[axis_at] // blocks).reshape((-1,) + (1,) * (len(shape) - 1 - axis_at))
    return level


def bell_draw(stream_key, extent, scale, limit, shards=(), held_as=jnp.bfloat16):
    entries = jax.random.normal(stream_key, extent, jnp.float32) * scale
    if len(shards) > 0:
        entries = shard_levels(stream_key, extent, shards, -0.22, 0.18) * entries
    return jnp.clip(entries, min=-limit, max=limit).astype(held_as)


def setup_inputs(seed: int = 0) -> dict:
    arg_keys = jax.random.split(jax.random.key(seed), 9)
    factor = bell_draw(arg_keys[0], (SLAB, NODES), NODES ** -0.5, 0.015625, ((0, 4), (1, 8)))
    panels = bell_draw(arg_keys[1], (NODES, SCENARIOS), 1.0, 6.0, ((0, 8), (1, 4)))
    base_demand = jnp.clip(jnp.exp(jax.random.uniform(arg_keys[2], (SLAB,), jnp.float32, math.log(0.3), math.log(3.0))), 0.3, 3.0)
    spread = jnp.clip(jnp.exp(jax.random.uniform(arg_keys[3], (SLAB,), jnp.float32, math.log(0.1), math.log(0.6))), 0.1, 0.6)
    head_base = bell_draw(arg_keys[4], (SLAB,), 2.0, 8.0, (), jnp.float32)
    head_drop = jnp.clip(jnp.exp(jax.random.uniform(arg_keys[5], (SLAB,), jnp.float32, math.log(0.2), math.log(1.0))), 0.2, 1.0)
    conductance = jnp.clip(jnp.exp(jax.random.uniform(arg_keys[6], (PIPES,), jnp.float32, math.log(0.3), math.log(1.5))), 0.3, 1.5)
    pipe_ends = place_ends(jax.random.randint(arg_keys[7], (PIPES, 2), 0, SLAB), jax.random.fold_in(arg_keys[7], 1), 0, SLAB - 1).astype(jnp.int32)
    return {"factor": factor, "panels": panels, "base_demand": base_demand, "spread": spread, "head_base": head_base, "head_drop": head_drop, "conductance": conductance, "pipe_ends": pipe_ends}


def reference(factor, panels, base_demand, spread, head_base, head_drop, conductance, pipe_ends):
    width = NODES // N_COL
    offset = NODES - SLAB

    def add_block(index, total):
        start = (index * width)
        block = lax.dynamic_slice_in_dim(factor, start, width, 1)
        draws = lax.dynamic_slice_in_dim(panels, start, width, 0)
        rows = lax.broadcasted_iota(jnp.int32, (SLAB, width), 0) + offset
        cols = lax.broadcasted_iota(jnp.int32, (SLAB, width), 1) + jnp.asarray(start).astype(jnp.int32)
        kept = jnp.where(cols <= rows, block, jnp.zeros_like(block))
        part = lax.dot_general(draws, kept, (((0,), (1,)), ((), ())), preferred_element_type=jnp.float32)
        return total + part

    scores = lax.fori_loop(0, N_COL, add_block, jnp.zeros((SCENARIOS, SLAB), jnp.float32))
    demand = base_demand * jnp.exp(spread * scores)
    heads = head_base - head_drop * demand
    starts = pipe_ends[:, 0]
    ends = pipe_ends[:, 1]
    diff = heads[:, starts] - heads[:, ends]
    flow = conductance * jnp.sign(diff) * jnp.abs(diff) ** 0.54
    inflow = jnp.zeros_like(demand).at[:, ends].add(flow).at[:, starts].add(-flow)
    return inflow - demand
```

```python
import functools

import jax
import jax.numpy as jnp
from jax import lax
from jax.experimental import pallas as pl
from jax.experimental.pallas import tpu as pltpu
from jax.sharding import PartitionSpec as P

NODES = 131072
LO = 256
PIPE_BLOCK = 1024
HALVES = 2


def split_bf16(x, parts):
    pieces = []
    for _ in range(parts):
        piece = x.astype(jnp.bfloat16).astype(jnp.float32)
        pieces.append(piece)
        x = x - piece
    return pieces


def residual_kernel(scores_ref, base_ref, spread_ref, head_ref, drop_ref, cond_ref, ends_ref, out_ref, heads_sc, demand_sc, acc_sc, hot_sc, lhs_sc):
    blocks, count, local = scores_ref.shape
    slab = blocks * local
    groups = slab // LO
    step = pl.program_id(0)
    rows = groups * count

    @pl.when(step == 0)
    def _():
        acc_sc[...] = jnp.zeros_like(acc_sc)
        for b in range(blocks):
            at = pl.ds(b * local, local)
            demand = base_ref[:, at] * jnp.exp(spread_ref[:, at] * scores_ref[b])
            demand_sc[:, at] = demand
            heads = head_ref[:, at] - drop_ref[:, at] * demand
            pieces = split_bf16(heads, 3)
            for p, piece in enumerate(pieces):
                for g in range(local // LO):
                    row = p * rows + (b * (local // LO) + g) * count
                    heads_sc[row : row + count, :] = piece[:, g * LO : (g + 1) * LO]

    width = ends_ref.shape[1]
    table = heads_sc[...].astype(jnp.bfloat16)
    lo_iota = lax.broadcasted_iota(jnp.int32, (LO, width), 0)
    picked = []
    groups_of = []
    for end in range(2):
        node = ends_ref[end : end + 1, :]
        lo = node & (LO - 1)
        hi = jnp.broadcast_to(node >> 8, (count, width))
        hot_sc[end] = jnp.where(lo_iota == lo, 1.0, 0.0).astype(jnp.bfloat16)
        found = jnp.dot(table, hot_sc[end], preferred_element_type=jnp.float32)
        found = found[:rows] + found[rows : 2 * rows] + found[2 * rows :]
        value = jnp.zeros((count, width), jnp.float32)
        for g in range(groups):
            value = jnp.where(hi == g, found[g * count : (g + 1) * count], value)
        picked.append(value)
        groups_of.append(hi)
    diff = picked[0] - picked[1]
    size = jnp.abs(diff)
    live = size > 0.0
    power = jnp.exp(0.54 * jnp.log(jnp.where(live, size, 1.0)))
    flow = cond_ref[...] * jnp.where(live, jnp.where(diff > 0.0, power, -power), 0.0)
    for end in range(2):
        pieces = split_bf16(-flow if end == 0 else flow, 2)
        spread_out = [
            jnp.where(groups_of[end] == g, piece, 0.0)
            for piece in pieces
            for g in range(groups)
        ]
        lhs_sc[end] = jnp.concatenate(spread_out, axis=0).astype(jnp.bfloat16)
        acc_sc[...] += lax.dot_general(hot_sc[end], lhs_sc[end], (((1,), (1,)), ((), ())), preferred_element_type=jnp.float32)

    @pl.when(step == pl.num_programs(0) - 1)
    def _():
        for g in range(groups):
            at = slice(g * LO, (g + 1) * LO)
            if g == 0:
                turned = acc_sc[...].T
            total = turned[g * count : (g + 1) * count, :] + turned[rows + g * count : rows + (g + 1) * count, :]
            out_ref[:, at] = total - demand_sc[:, at]


def residual(scores, base_demand, spread, head_base, head_drop, conductance, pipe_ends):
    blocks, count, local = scores.shape
    slab = blocks * local
    pipes = conductance.shape[0]
    rows = slab // LO * count
    whole = lambda shape: pl.BlockSpec(shape, lambda e: (0,) * len(shape))
    return pl.pallas_call(
        residual_kernel,
        grid=(pipes // PIPE_BLOCK,),
        out_shape=jax.ShapeDtypeStruct((count, slab), jnp.float32),
        in_specs=[
            whole((blocks, count, local)),
            whole((1, slab)),
            whole((1, slab)),
            whole((1, slab)),
            whole((1, slab)),
            pl.BlockSpec((1, PIPE_BLOCK), lambda e: (0, e)),
            pl.BlockSpec((2, PIPE_BLOCK), lambda e: (0, e)),
        ],
        out_specs=whole((count, slab)),
        scratch_shapes=[
            pltpu.VMEM((3 * rows, LO), jnp.float32),
            pltpu.VMEM((count, slab), jnp.float32),
            pltpu.VMEM((LO, 2 * rows), jnp.float32),
            pltpu.VMEM((2, LO, PIPE_BLOCK), jnp.bfloat16),
            pltpu.VMEM((2, 2 * rows, PIPE_BLOCK), jnp.bfloat16),
        ],
        compiler_params=pltpu.CompilerParams(dimension_semantics=("arbitrary",), vmem_limit_bytes=48 * 1024 * 1024),
    )(
        scores,
        base_demand[None, :],
        spread[None, :],
        head_base[None, :],
        head_drop[None, :],
        conductance[None, :],
        pipe_ends.T,
    )


CHUNKS = 4
MESH = pl.DeviceIdType.MESH


def gather_kernel(panels_ref, factor_ref, out_ref, draws, kept, own_sem, factor_sem, send_sem, recv_sem):
    drawn, width = panels_ref.shape
    local_rows = factor_ref.shape[0]
    half = drawn // 2
    span = width // CHUNKS
    me = lax.axis_index("row")
    beside = me + 1 - 2 * (me % 2)
    across = me + 2 - 4 * (me // 2)
    order = (me, beside, across, 3 - me)

    barrier = pltpu.get_barrier_semaphore()
    for peer in (beside, across):
        pl.semaphore_signal(barrier, inc=1, device_id={"row": peer}, device_id_type=MESH)
    pl.semaphore_wait(barrier, 2)

    def at(block, part, c):
        return draws.at[pl.ds(block * drawn + part * half, half), pl.ds(c * span, span)]

    def send(kind, c, source, target, peer):
        return pltpu.make_async_remote_copy(
            src_ref=source,
            dst_ref=target,
            send_sem=send_sem.at[kind, c],
            recv_sem=recv_sem.at[kind, c],
            device_id={"row": peer},
            device_id_type=MESH,
        )

    def mine(part, c):
        return panels_ref.at[pl.ds(part * half, half), pl.ds(c * span, span)]

    sends = []
    for c in range(CHUNKS):
        sends.append(
            (
                send(0, c, mine(0, c), at(1, 0, c), beside),
                send(1, c, mine(1, c), at(2, 1, c), across),
                send(2, c, mine(1, c), at(1, 1, c), beside),
                send(3, c, mine(0, c), at(2, 0, c), across),
                send(4, c, at(1, 0, c), at(3, 0, c), across),
                send(5, c, at(2, 1, c), at(3, 1, c), beside),
            )
        )

    def start(c):
        for copy in sends[c][:4]:
            copy.start()

    def forward(c):
        sends[c][0].wait_recv()
        sends[c][4].start()
        sends[c][1].wait_recv()
        sends[c][5].start()

    start(0)
    start(1)
    own = pltpu.make_async_copy(panels_ref, draws.at[pl.ds(0, drawn), :], own_sem)
    own.start()
    loads = []
    for c in range(CHUNKS):
        piece = pl.ds(c * span, span)
        loads.append(pltpu.make_async_copy(factor_ref.at[:, piece], kept.at[:, piece], factor_sem.at[c]))
        loads[c].start()
    own.wait()

    first_row = NODES - lax.axis_size("row") * local_rows + me * local_rows
    strip = 64
    tile = 256
    forward(0)
    for c in range(CHUNKS):
        if c + 2 < CHUNKS:
            start(c + 2)
        first_col = lax.axis_index("col") * width + c * span
        loads[c].wait()

        @pl.when(first_col + span > first_row)
        def _():
            def mask(t, carry):
                where = pl.ds(pl.multiple_of(t * strip, strip), strip)
                block = kept[where, c * span : (c + 1) * span].astype(jnp.float32)
                row = lax.broadcasted_iota(jnp.int32, block.shape, 0) + (first_row + t * strip)
                col = lax.broadcasted_iota(jnp.int32, block.shape, 1) + first_col
                block = jnp.where(col <= row, block, 0.0)
                kept[where, c * span : (c + 1) * span] = block.astype(jnp.bfloat16)
                return carry

            lax.fori_loop(0, local_rows // strip, mask, 0)

        if c + 1 < CHUNKS:
            forward(c + 1)
        for kind in range(2, 6):
            sends[c][kind].wait_recv()

        def multiply(t, carry):
            where = pl.ds(pl.multiple_of(t * tile, tile), tile)
            found = lax.dot_general(
                draws[:, c * span : (c + 1) * span],
                kept[where, c * span : (c + 1) * span],
                (((1,), (1,)), ((), ())),
                preferred_element_type=jnp.float32,
            )
            for block in range(4):
                rows = pl.ds(pl.multiple_of(order[block] * drawn, drawn), drawn)
                piece = found[block * drawn : (block + 1) * drawn]
                if c == 0:
                    out_ref[rows, where] = piece
                else:
                    out_ref[rows, where] += piece
            return carry

        lax.fori_loop(0, local_rows // tile, multiply, 0)
    for c in range(CHUNKS):
        for copy in sends[c]:
            copy.wait_send()


def gathered_scores(draws, factor):
    drawn, width = draws.shape
    local_rows = factor.shape[0]
    return pl.pallas_call(
        gather_kernel,
        out_shape=jax.ShapeDtypeStruct((4 * drawn, local_rows), jnp.float32),
        in_specs=[pl.BlockSpec(memory_space=pl.ANY)] * 2,
        out_specs=pl.BlockSpec(memory_space=pltpu.VMEM),
        scratch_shapes=[
            pltpu.VMEM((4 * drawn, width), jnp.bfloat16),
            pltpu.VMEM((local_rows, width), jnp.bfloat16),
            pltpu.SemaphoreType.DMA,
            pltpu.SemaphoreType.DMA((CHUNKS,)),
            pltpu.SemaphoreType.DMA((6, CHUNKS)),
            pltpu.SemaphoreType.DMA((6, CHUNKS)),
        ],
        compiler_params=pltpu.CompilerParams(collective_id=0, has_side_effects=True, vmem_limit_bytes=56 * 1024 * 1024),
    )(draws, factor)


def shards(factor, panels, base_demand, spread, head_base, head_drop, conductance, pipe_ends):
    local_rows, width = factor.shape
    n_row = lax.axis_size("row")
    n_col = lax.axis_size("col")
    if n_row == 4:
        partial_scores = gathered_scores(panels.T, factor)
        summed = lax.psum_scatter(partial_scores, "col", scatter_dimension=0, tiled=True)
        shares = summed.reshape(n_row, -1, local_rows)
        scores = lax.all_to_all(shares, "row", split_axis=0, concat_axis=0, tiled=True)
        return residual(scores, base_demand, spread, head_base, head_drop, conductance, pipe_ends)
    slab = local_rows * n_row
    offset = NODES - slab
    rows = lax.broadcasted_iota(jnp.int32, factor.shape, 0) + offset + lax.axis_index("row") * local_rows
    cols = lax.broadcasted_iota(jnp.int32, factor.shape, 1) + lax.axis_index("col") * width
    kept = jnp.where(cols <= rows, factor, jnp.zeros_like(factor))
    drawn = panels.shape[1]
    count = drawn // n_col
    part = count // HALVES
    draws = panels.T.reshape(drawn // count, HALVES, part, width)
    sums = []
    for h in range(HALVES):
        mine = draws[:, h].reshape(drawn // HALVES, width)
        every = lax.all_gather(mine, "row", axis=0, tiled=True)
        partial_scores = lax.dot_general(every, kept, (((1,), (1,)), ((), ())), preferred_element_type=jnp.float32)
        sums.append(lax.psum_scatter(partial_scores, "col", scatter_dimension=0, tiled=True))
    stacked = jnp.stack([s.reshape(n_row, part, local_rows) for s in sums], axis=1)
    stacked = stacked.reshape(n_row, count, local_rows)
    scores = lax.all_to_all(stacked, "row", split_axis=0, concat_axis=0, tiled=True)
    return residual(scores, base_demand, spread, head_base, head_drop, conductance, pipe_ends)


def solution(mesh):
    return jax.shard_map(
        shards,
        mesh=mesh,
        in_specs=(P("row", "col"), P("col", "row"), P(), P(), P(), P(), P(), P()),
        out_specs=P(("col", "row"), None),
        check_vma=False,
    )
```

```python
import functools

import jax
import jax.numpy as jnp
from jax import lax
from jax.experimental import pallas as pl
from jax.experimental.pallas import tpu as pltpu
from jax.sharding import PartitionSpec as P

NODES = 131072
LO = 256
PIPE_BLOCK = 1024
HALVES = 2


def split_bf16(x, parts):
    pieces = []
    for _ in range(parts):
        piece = x.astype(jnp.bfloat16).astype(jnp.float32)
        pieces.append(piece)
        x = x - piece
    return pieces


def residual_kernel(scores_ref, base_ref, spread_ref, head_ref, drop_ref, cond_ref, ends_ref, out_ref, heads_sc, demand_sc, acc_sc, hot_sc, lhs_sc):
    blocks, count, local = scores_ref.shape
    slab = blocks * local
    groups = slab // LO
    step = pl.program_id(0)
    rows = groups * count

    @pl.when(step == 0)
    def _():
        acc_sc[...] = jnp.zeros_like(acc_sc)
        for b in range(blocks):
            at = pl.ds(b * local, local)
            demand = base_ref[:, at] * jnp.exp(spread_ref[:, at] * scores_ref[b])
            demand_sc[:, at] = demand
            heads = head_ref[:, at] - drop_ref[:, at] * demand
            pieces = split_bf16(heads, 3)
            for p, piece in enumerate(pieces):
                for g in range(local // LO):
                    row = p * rows + (b * (local // LO) + g) * count
                    heads_sc[row : row + count, :] = piece[:, g * LO : (g + 1) * LO]

    width = ends_ref.shape[1]
    table = heads_sc[...].astype(jnp.bfloat16)
    lo_iota = lax.broadcasted_iota(jnp.int32, (LO, width), 0)
    picked = []
    groups_of = []
    for end in range(2):
        node = ends_ref[end : end + 1, :]
        lo = node & (LO - 1)
        hi = jnp.broadcast_to(node >> 8, (count, width))
        hot_sc[end] = jnp.where(lo_iota == lo, 1.0, 0.0).astype(jnp.bfloat16)
        found = jnp.dot(table, hot_sc[end], preferred_element_type=jnp.float32)
        found = found[:rows] + found[rows : 2 * rows] + found[2 * rows :]
        value = jnp.zeros((count, width), jnp.float32)
        for g in range(groups):
            value = jnp.where(hi == g, found[g * count : (g + 1) * count], value)
        picked.append(value)
        groups_of.append(hi)
    diff = picked[0] - picked[1]
    size = jnp.abs(diff)
    live = size > 0.0
    power = jnp.exp(0.54 * jnp.log(jnp.where(live, size, 1.0)))
    flow = cond_ref[...] * jnp.where(live, jnp.where(diff > 0.0, power, -power), 0.0)
    for end in range(2):
        pieces = split_bf16(-flow if end == 0 else flow, 2)
        spread_out = [
            jnp.where(groups_of[end] == g, piece, 0.0)
            for piece in pieces
            for g in range(groups)
        ]
        lhs_sc[end] = jnp.concatenate(spread_out, axis=0).astype(jnp.bfloat16)
        acc_sc[...] += lax.dot_general(hot_sc[end], lhs_sc[end], (((1,), (1,)), ((), ())), preferred_element_type=jnp.float32)

    @pl.when(step == pl.num_programs(0) - 1)
    def _():
        for g in range(groups):
            at = slice(g * LO, (g + 1) * LO)
            if g == 0:
                turned = acc_sc[...].T
            total = turned[g * count : (g + 1) * count, :] + turned[rows + g * count : rows + (g + 1) * count, :]
            out_ref[:, at] = total - demand_sc[:, at]


def residual(scores, base_demand, spread, head_base, head_drop, conductance, pipe_ends):
    blocks, count, local = scores.shape
    slab = blocks * local
    pipes = conductance.shape[0]
    rows = slab // LO * count
    whole = lambda shape: pl.BlockSpec(shape, lambda e: (0,) * len(shape))
    return pl.pallas_call(
        residual_kernel,
        grid=(pipes // PIPE_BLOCK,),
        out_shape=jax.ShapeDtypeStruct((count, slab), jnp.float32),
        in_specs=[
            whole((blocks, count, local)),
            whole((1, slab)),
            whole((1, slab)),
            whole((1, slab)),
            whole((1, slab)),
            pl.BlockSpec((1, PIPE_BLOCK), lambda e: (0, e)),
            pl.BlockSpec((2, PIPE_BLOCK), lambda e: (0, e)),
        ],
        out_specs=whole((count, slab)),
        scratch_shapes=[
            pltpu.VMEM((3 * rows, LO), jnp.float32),
            pltpu.VMEM((count, slab), jnp.float32),
            pltpu.VMEM((LO, 2 * rows), jnp.float32),
            pltpu.VMEM((2, LO, PIPE_BLOCK), jnp.bfloat16),
            pltpu.VMEM((2, 2 * rows, PIPE_BLOCK), jnp.bfloat16),
        ],
        compiler_params=pltpu.CompilerParams(dimension_semantics=("arbitrary",), vmem_limit_bytes=48 * 1024 * 1024),
    )(
        scores,
        base_demand[None, :],
        spread[None, :],
        head_base[None, :],
        head_drop[None, :],
        conductance[None, :],
        pipe_ends.T,
    )


CHUNKS = 4
MESH = pl.DeviceIdType.MESH


def gather_kernel(panels_ref, factor_ref, out_ref, draws, kept, own_sem, factor_sem, send_sem, recv_sem):
    drawn, width = panels_ref.shape
    local_rows = factor_ref.shape[0]
    half = drawn // 2
    span = width // CHUNKS
    me = lax.axis_index("row")
    beside = me + 1 - 2 * (me % 2)
    across = me + 2 - 4 * (me // 2)
    order = (me, beside, across, 3 - me)

    barrier = pltpu.get_barrier_semaphore()
    for peer in (beside, across):
        pl.semaphore_signal(barrier, inc=1, device_id={"row": peer}, device_id_type=MESH)
    pl.semaphore_wait(barrier, 2)

    def at(block, part, c):
        return draws.at[pl.ds(block * drawn + part * half, half), pl.ds(c * span, span)]

    def send(kind, c, source, target, peer):
        return pltpu.make_async_remote_copy(
            src_ref=source,
            dst_ref=target,
            send_sem=send_sem.at[kind, c],
            recv_sem=recv_sem.at[kind, c],
            device_id={"row": peer},
            device_id_type=MESH,
        )

    def mine(part, c):
        return panels_ref.at[pl.ds(part * half, half), pl.ds(c * span, span)]

    sends = []
    for c in range(CHUNKS):
        sends.append(
            (
                send(0, c, mine(0, c), at(1, 0, c), beside),
                send(1, c, mine(1, c), at(2, 1, c), across),
                send(2, c, mine(1, c), at(1, 1, c), beside),
                send(3, c, mine(0, c), at(2, 0, c), across),
                send(4, c, at(1, 0, c), at(3, 0, c), across),
                send(5, c, at(2, 1, c), at(3, 1, c), beside),
            )
        )

    def start(c):
        for copy in sends[c][:4]:
            copy.start()

    def forward(c):
        sends[c][0].wait_recv()
        sends[c][4].start()
        sends[c][1].wait_recv()
        sends[c][5].start()

    start(0)
    start(1)
    own = pltpu.make_async_copy(panels_ref, draws.at[pl.ds(0, drawn), :], own_sem)
    own.start()
    loads = []
    for c in range(CHUNKS):
        piece = pl.ds(c * span, span)
        loads.append(pltpu.make_async_copy(factor_ref.at[:, piece], kept.at[:, piece], factor_sem.at[c]))
        loads[c].start()
    own.wait()

    first_row = NODES - lax.axis_size("row") * local_rows + me * local_rows
    strip = 64
    tile = 256
    forward(0)
    for c in range(CHUNKS):
        if c + 2 < CHUNKS:
            start(c + 2)
        first_col = lax.axis_index("col") * width + c * span
        loads[c].wait()

        @pl.when(first_col + span > first_row)
        def _():
            def mask(t, carry):
                where = pl.ds(pl.multiple_of(t * strip, strip), strip)
                block = kept[where, c * span : (c + 1) * span].astype(jnp.float32)
                row = lax.broadcasted_iota(jnp.int32, block.shape, 0) + (first_row + t * strip)
                col = lax.broadcasted_iota(jnp.int32, block.shape, 1) + first_col
                block = jnp.where(col <= row, block, 0.0)
                kept[where, c * span : (c + 1) * span] = block.astype(jnp.bfloat16)
                return carry

            lax.fori_loop(0, local_rows // strip, mask, 0)

        if c + 1 < CHUNKS:
            forward(c + 1)
        for kind in range(2, 6):
            sends[c][kind].wait_recv()

        def multiply(t, carry):
            where = pl.ds(pl.multiple_of(t * tile, tile), tile)
            found = lax.dot_general(
                draws[:, c * span : (c + 1) * span],
                kept[where, c * span : (c + 1) * span],
                (((1,), (1,)), ((), ())),
                preferred_element_type=jnp.float32,
            )
            for block in range(4):
                rows = pl.ds(pl.multiple_of(order[block] * drawn, drawn), drawn)
                piece = found[block * drawn : (block + 1) * drawn]
                if c == 0:
                    out_ref[rows, where] = piece
                else:
                    out_ref[rows, where] += piece
            return carry

        lax.fori_loop(0, local_rows // tile, multiply, 0)
    for c in range(CHUNKS):
        for copy in sends[c]:
            copy.wait_send()


def gathered_scores(draws, factor):
    drawn, width = draws.shape
    local_rows = factor.shape[0]
    return pl.pallas_call(
        gather_kernel,
        out_shape=jax.ShapeDtypeStruct((4 * drawn, local_rows), jnp.float32),
        in_specs=[pl.BlockSpec(memory_space=pl.ANY)] * 2,
        out_specs=pl.BlockSpec(memory_space=pltpu.VMEM),
        scratch_shapes=[
            pltpu.VMEM((4 * drawn, width), jnp.bfloat16),
            pltpu.VMEM((local_rows, width), jnp.bfloat16),
            pltpu.SemaphoreType.DMA,
            pltpu.SemaphoreType.DMA((CHUNKS,)),
            pltpu.SemaphoreType.DMA((6, CHUNKS)),
            pltpu.SemaphoreType.DMA((6, CHUNKS)),
        ],
        compiler_params=pltpu.CompilerParams(collective_id=0, has_side_effects=True, vmem_limit_bytes=56 * 1024 * 1024),
    )(draws, factor)


def reduce_kernel(part_ref, out_ref, paired, landed, total, got, pair_send, pair_recv, z_send, z_recv, row_send, row_recv):
    chips, share, _ = paired.shape
    n_row, count, _ = got.shape
    me = lax.axis_index("row")
    column = lax.axis_index("col")
    z = column // 2
    core = column % 2
    sibling = column + 1 - 2 * core

    barrier = pltpu.get_barrier_semaphore()
    peers = [{"col": sibling}]
    peers += [{"col": ((z + d) % chips) * 2 + core} for d in range(1, chips)]
    peers += [{"row": (me + d) % n_row} for d in range(1, n_row)]
    for peer in peers:
        pl.semaphore_signal(barrier, inc=1, device_id=peer, device_id_type=MESH)
    pl.semaphore_wait(barrier, len(peers))

    def block(d, side):
        start = (((z + d) % chips) * 2 + side) * share
        return pl.ds(pl.multiple_of(start, share), share)

    order = list(range(1, chips)) + [0]
    pairs = {}
    for d in order:
        pairs[d] = pltpu.make_async_remote_copy(
            src_ref=part_ref.at[block(d, 1 - core), :],
            dst_ref=paired.at[d],
            send_sem=pair_send.at[d],
            recv_sem=pair_recv.at[d],
            device_id={"col": sibling},
            device_id_type=MESH,
        )
        pairs[d].start()
    hops = []
    for d in order:
        pairs[d].wait_recv()
        if d == 0:
            total[...] = paired[0] + part_ref[block(0, core), :]
            continue
        paired[d] = paired[d] + part_ref[block(d, core), :]
        hop = pltpu.make_async_remote_copy(
            src_ref=paired.at[d],
            dst_ref=landed.at[d - 1],
            send_sem=z_send.at[d - 1],
            recv_sem=z_recv.at[d - 1],
            device_id={"col": ((z + d) % chips) * 2 + core},
            device_id_type=MESH,
        )
        hop.start()
        hops.append(hop)
    for d, hop in enumerate(hops):
        hop.wait_recv()
        total[...] = total[...] + landed[d]
    moves = []
    for d in range(1, n_row):
        target = (me + d) % n_row
        move = pltpu.make_async_remote_copy(
            src_ref=total.at[pl.ds(pl.multiple_of(target * count, count), count), :],
            dst_ref=got.at[me],
            send_sem=row_send.at[d - 1],
            recv_sem=row_recv.at[d - 1],
            device_id={"row": target},
            device_id_type=MESH,
        )
        move.start()
        moves.append(move)
    out_ref[me] = total[pl.ds(pl.multiple_of(me * count, count), count), :]
    for d, move in enumerate(moves):
        move.wait_recv()
        source = (me + n_row - d - 1) % n_row
        out_ref[source] = got[source]
    for d in order:
        pairs[d].wait_send()
    for copy in hops + moves:
        copy.wait_send()


def reduced_scores(partial_scores, n_row, n_col):
    scenarios, local_rows = partial_scores.shape
    chips = n_col // 2
    share = scenarios // n_col
    count = share // n_row
    return pl.pallas_call(
        reduce_kernel,
        out_shape=jax.ShapeDtypeStruct((n_row, count, local_rows), jnp.float32),
        in_specs=[pl.BlockSpec(memory_space=pltpu.VMEM)],
        out_specs=pl.BlockSpec(memory_space=pltpu.VMEM),
        scratch_shapes=[
            pltpu.VMEM((chips, share, local_rows), jnp.float32),
            pltpu.VMEM((chips - 1, share, local_rows), jnp.float32),
            pltpu.VMEM((share, local_rows), jnp.float32),
            pltpu.VMEM((n_row, count, local_rows), jnp.float32),
            pltpu.SemaphoreType.DMA((chips,)),
            pltpu.SemaphoreType.DMA((chips,)),
            pltpu.SemaphoreType.DMA((chips - 1,)),
            pltpu.SemaphoreType.DMA((chips - 1,)),
            pltpu.SemaphoreType.DMA((n_row - 1,)),
            pltpu.SemaphoreType.DMA((n_row - 1,)),
        ],
        compiler_params=pltpu.CompilerParams(collective_id=1, has_side_effects=True, vmem_limit_bytes=32 * 1024 * 1024),
    )(partial_scores)


def shards(factor, panels, base_demand, spread, head_base, head_drop, conductance, pipe_ends):
    local_rows, width = factor.shape
    n_row = lax.axis_size("row")
    n_col = lax.axis_size("col")
    if n_row == 4:
        partial_scores = gathered_scores(panels.T, factor)
        scores = reduced_scores(partial_scores, n_row, n_col)
        return residual(scores, base_demand, spread, head_base, head_drop, conductance, pipe_ends)
    slab = local_rows * n_row
    offset = NODES - slab
    rows = lax.broadcasted_iota(jnp.int32, factor.shape, 0) + offset + lax.axis_index("row") * local_rows
    cols = lax.broadcasted_iota(jnp.int32, factor.shape, 1) + lax.axis_index("col") * width
    kept = jnp.where(cols <= rows, factor, jnp.zeros_like(factor))
    drawn = panels.shape[1]
    count = drawn // n_col
    part = count // HALVES
    draws = panels.T.reshape(drawn // count, HALVES, part, width)
    sums = []
    for h in range(HALVES):
        mine = draws[:, h].reshape(drawn // HALVES, width)
        every = lax.all_gather(mine, "row", axis=0, tiled=True)
        partial_scores = lax.dot_general(every, kept, (((1,), (1,)), ((), ())), preferred_element_type=jnp.float32)
        sums.append(lax.psum_scatter(partial_scores, "col", scatter_dimension=0, tiled=True))
    stacked = jnp.stack([s.reshape(n_row, part, local_rows) for s in sums], axis=1)
    stacked = stacked.reshape(n_row, count, local_rows)
    scores = lax.all_to_all(stacked, "row", split_axis=0, concat_axis=0, tiled=True)
    return residual(scores, base_demand, spread, head_base, head_drop, conductance, pipe_ends)


def solution(mesh):
    return jax.shard_map(
        shards,
        mesh=mesh,
        in_specs=(P("row", "col"), P("col", "row"), P(), P(), P(), P(), P(), P()),
        out_specs=P(("col", "row"), None),
        check_vma=False,
    )
```
